32 devices in a mesh: sections: 4 (over y, x), cache: 4 (over z), heads: 2 (over core).
Axes of the slice: x: 2, y: 2, z: 4, core: 2. Of those that a mesh axis runs over, the one named last changes fastest.
Arguments:
- hidden: bfloat16 [4, 1024, 2048], P('sections', 'cache'), may hold values from -6 to 6
- norm_gain: float32 [4, 2048], P('sections'), may hold values from 0.1 to 1.9
- w_query: bfloat16 [4, 2048, 4096], P('sections', None, 'heads'), may hold values from -0.125 to 0.125
- query_gain: float32 [4, 128], P('sections'), may hold values from 0.1 to 1.9
- w_output: bfloat16 [4, 4096, 2048], P('sections', 'heads'), may hold values from -0.09375 to 0.09375
- key_cache: bfloat16 [4, 128, 64, 512], P('sections', 'cache', None, 'heads'), may hold values from -6 to 6
- value_cache: bfloat16 [4, 128, 64, 512], P('sections', 'cache', None, 'heads'), may hold values from -6 to 6
- key_scale: float32 [4, 128, 4], P('sections', 'cache', 'heads'), may hold values from 0.5 to 120
- value_scale: float32 [4, 128, 4], P('sections', 'cache', 'heads'), may hold values from 0.5 to 2
- page_table: int32 [128], replicated, may hold values from 0 to 127, as said below
- page_tokens: int32 [128], replicated, may hold values from 1 to 64
- page_list: int32 [4, 8, 16], P('sections'), may hold values from 0 to 127, as said below
- list_len: int32 [4, 8], P('sections'), may hold values from 8 to 16, as said below
Outputs:
- mixed: bfloat16 [4, 1024, 2048], P('sections', 'cache', 'heads')
The draws below stay inside these ranges and needn't reach their ends.
Inputs may be any that keep to these rules, and one draw needn't show every extreme that they name: `page_table`: A permutation of the 128 slots; slot // 32 is the cache index that holds the page. `page_list`: the 16 entries of a block are distinct logical pages; among them at most 8 have their slot on any one cache index, and in every block some cache index holds exactly 8 of them. Entries of a list from list_len on are unused; some block uses all 16 entries.
All inputs are finite; a program needn't handle non-finite values.
Results may differ from the reference program's by a relative error of at most 0.008.
The reference program's roundings to bfloat16 on the way (of `normed`, `queries`, `scaled`, `attended` and `updated`) count: a program that leaves them out, or rounds other values in their place, can miss the bound.
Values may be sent and summed in bfloat16 or wider, within the bound.
A program may use at most 128 MiB of HBM per device.

```python
import math
import jax
import jax.numpy as jnp
from jax import lax

D = 2048
Q_HEADS = 32
KV_HEADS = 4
HEAD_DIM = 128
QBLOCK = 128
PAGE = 64
PAGES_DEV = 32
MOST = 8
LIST = 16
PAGES = 128
BLOCKS = 8
ROWS = 1024
N_SECTIONS = 4
N_CACHE = 4


def page_layout(key):
    slot_of_page = jax.random.permutation(jax.random.fold_in(key, 11), PAGES).astype(jnp.int32)
    page_of_slot = jnp.argsort(slot_of_page).astype(jnp.int32)
    remaining = LIST - MOST
    base_count = remaining // (N_CACHE - 1)
    leftover = remaining % (N_CACHE - 1)
    pair_count = (N_CACHE - 1) // 2
    headroom = base_count // 2
    shard_ids = jnp.arange(N_CACHE, dtype=jnp.int32)
    slot_ids = jnp.arange(PAGES, dtype=jnp.int32)
    slot_shard = slot_ids // PAGES_DEV

    def one_list(block_key):
        busy_shard = jax.random.randint(jax.random.fold_in(block_key, 1), (), 0, N_CACHE)
        spread = jax.random.permutation(jax.random.fold_in(block_key, 2), N_CACHE - 1).astype(jnp.int32)
        others = base_count + (spread < leftover).astype(jnp.int32)
        amounts = jax.random.randint(jax.random.fold_in(block_key, 3), (pair_count,), 0, headroom + 1).astype(jnp.int32)
        moves = jnp.zeros((N_CACHE - 1,), jnp.int32)
        moves = moves.at[0:2 * pair_count:2].add(amounts).at[1:2 * pair_count:2].add(-amounts)
        others = others + moves
        position = jnp.clip(shard_ids - (shard_ids > busy_shard).astype(jnp.int32), 0, N_CACHE - 2)
        quota = jnp.where(shard_ids == busy_shard, MOST, others[position])
        ranking = jax.random.permutation(jax.random.fold_in(block_key, 4), PAGES).astype(jnp.int32)
        sorted_order = jnp.argsort(slot_shard * PAGES + ranking)
        within = jnp.argsort(sorted_order).astype(jnp.int32) - slot_shard * PAGES_DEV
        chosen = (within < quota[slot_shard]).astype(jnp.int32)
        shuffle = jax.random.permutation(jax.random.fold_in(block_key, 5), PAGES).astype(jnp.int32)
        picked = jnp.argsort((1 - chosen) * PAGES + shuffle)[:LIST]
        return page_of_slot[picked]
    block_keys = jax.vmap(lambda index: jax.random.fold_in(key, index))(jnp.arange(N_SECTIONS * BLOCKS))
    lists = jax.vmap(one_list)(block_keys).reshape(N_SECTIONS, BLOCKS, LIST)
    return (slot_of_page, lists)


def draw_page_table(key, part):
    return page_layout(key)[0].astype(jnp.int32)


def draw_page_list(key, part):
    return page_layout(key)[1].astype(jnp.int32)


def draw_list_len(key, part):
    lengths = jax.random.randint(jax.random.fold_in(key, 21), (N_SECTIONS * BLOCKS,), LIST // 2, LIST + 1)
    full_block = jax.random.randint(jax.random.fold_in(key, 22), (), 0, N_SECTIONS * BLOCKS)
    flat = jnp.where(jnp.arange(N_SECTIONS * BLOCKS) == full_block, LIST, lengths)
    return flat.reshape(N_SECTIONS, BLOCKS).astype(jnp.int32)


def draw_key_scale(key, part):
    shape = (N_SECTIONS, PAGES, KV_HEADS)
    scales = jnp.exp(jax.random.uniform(jax.random.fold_in(key, 31), shape, jnp.float32, math.log(0.5), math.log(2.0)))
    return scales.astype(jnp.float32)


def place_ends(drawn, own_key, smallest, high):
    dims = drawn.shape
    spot = [jax.random.randint(jax.random.fold_in(own_key, axis), (), 0, dims[axis]) for axis in range(len(dims))]
    drawn = drawn.at[tuple(spot)].set(smallest)
    longest = dims.index(max(dims))
    spot[longest] = (spot[longest] + 1) % dims[longest]
    return drawn.at[tuple(spot)].set(high)


def block_scale(own_key, shape, shards, low, largest):
    loudness = 1.0
    for dim, shards_of in shards:
        steps = jax.random.uniform(jax.random.fold_in(jax.random.fold_in(own_key, 6), dim), (shards_of,), jnp.float32, low / len(shards), largest / len(shards))
        loudness = loudness * jnp.repeat(jnp.exp(steps), shape[dim] // shards_of).reshape((-1,) + (1,) * (len(shape) - 1 - dim))
    return loudness


def normal_values(stream_key, dims, width, reach, cuts=(), held_as=jnp.bfloat16):
    values = jax.random.normal(stream_key, dims, jnp.float32) * width
    if len(cuts) > 0:
        values = block_scale(stream_key, dims, cuts, -0.22, 0.18) * values
    return jnp.clip(values, min=-reach, max=reach).astype(held_as)


def setup_inputs(seed: int = 0) -> dict:
    streams_of = jax.random.split(jax.random.key(seed), 14)
    return {
        "hidden": normal_values(streams_of[0], (N_SECTIONS, ROWS, D), 1.0, 6.0, ((0, 4), (1, 4))),
        "norm_gain": jnp.clip(1.0 + 0.18 * jax.random.normal(streams_of[1], (N_SECTIONS, D), jnp.float32), 0.1, 1.9),
        "w_query": normal_values(streams_of[2], (N_SECTIONS, D, Q_HEADS * HEAD_DIM), D ** -0.5, 0.125, ((0, 4), (2, 2))),
        "query_gain": jnp.clip(1.0 + 0.18 * jax.random.normal(streams_of[3], (N_SECTIONS, HEAD_DIM), jnp.float32), 0.1, 1.9),
        "w_output": normal_values(streams_of[4], (N_SECTIONS, Q_HEADS * HEAD_DIM, D), (Q_HEADS * HEAD_DIM) ** -0.5, 0.09375, ((0, 4), (1, 2))),
        "key_cache": normal_values(streams_of[5], (N_SECTIONS, PAGES, PAGE, KV_HEADS * HEAD_DIM), 1.0, 6.0, ((0, 4), (1, 4), (3, 2))),
        "value_cache": normal_values(streams_of[6], (N_SECTIONS, PAGES, PAGE, KV_HEADS * HEAD_DIM), 1.0, 6.0, ((0, 4), (1, 4), (3, 2))),
        "key_scale": draw_key_scale(jax.random.fold_in(streams_of[13], 71), 0),
        "value_scale": jnp.clip(jnp.exp(math.log(2.0) - 1.3862944 * jax.random.uniform(streams_of[8], (N_SECTIONS, PAGES, KV_HEADS), jnp.float32) ** block_scale(streams_of[8], (N_SECTIONS, PAGES, KV_HEADS), ((0, 4), (1, 4), (2, 2)), -0.2, 0.2)), 0.5, 2.0),
        "page_table": draw_page_table(jax.random.fold_in(streams_of[13], 71), 0),
        "page_tokens": place_ends(jax.random.randint(streams_of[10], (PAGES,), 1, PAGE + 1), jax.random.fold_in(streams_of[10], 1), 1, PAGE).astype(jnp.int32),
        "page_list": draw_page_list(jax.random.fold_in(streams_of[13], 71), 0),
        "list_len": draw_list_len(jax.random.fold_in(streams_of[13], 71), 0),
    }


tiny_eps = 1e-06
masked_score = -1e+30

def one_section(hidden_rows, gain_row, query_weight, head_gain, output_weight, key_pages, value_pages, key_scales, value_scales, page_table, page_tokens, lists, lengths):
    inputs = hidden_rows.astype(jnp.float32)
    inverse = lax.rsqrt(lax.optimization_barrier(jnp.mean(inputs * inputs, axis=-1, keepdims=True)) + tiny_eps)
    normed = (inputs * inverse * gain_row).astype(jnp.bfloat16)
    projected = jnp.dot(normed, query_weight, preferred_element_type=jnp.float32).reshape(ROWS, Q_HEADS, HEAD_DIM)
    head_inverse = lax.rsqrt(lax.optimization_barrier(jnp.mean(projected * projected, axis=-1, keepdims=True)) + tiny_eps)
    queries = (projected * head_inverse * head_gain / math.sqrt(HEAD_DIM)).astype(jnp.bfloat16)
    group_size = Q_HEADS // KV_HEADS
    queries = queries.reshape(BLOCKS, QBLOCK, KV_HEADS, group_size, HEAD_DIM)

    def one_block(block_args):
        block_queries, entries, length = block_args
        slots = page_table[entries]
        counts = page_tokens[entries]
        key_rows = key_pages[slots].reshape(LIST * PAGE, KV_HEADS, HEAD_DIM).astype(jnp.float32)
        value_rows = value_pages[slots].reshape(LIST * PAGE, KV_HEADS, HEAD_DIM).astype(jnp.float32)
        key_factor = jnp.repeat(key_scales[slots], PAGE, axis=0).T
        value_factor = jnp.repeat(value_scales[slots], PAGE, axis=0).T
        entry_ids = jnp.arange(LIST, dtype=jnp.int32)
        token_ids = jnp.arange(PAGE, dtype=jnp.int32)
        live_mask = ((entry_ids[:, None] < length) & (token_ids[None, :] < counts[:, None])).reshape(LIST * PAGE)
        scores = jnp.einsum('rgjd,tgd->gjrt', block_queries.astype(jnp.float32), key_rows) * key_factor[:, None, None, :]
        scores = jnp.where(live_mask, scores, masked_score)
        top_score = lax.optimization_barrier(jnp.max(scores, axis=-1, keepdims=True))
        weights = jnp.where(live_mask, jnp.exp(scores - top_score), 0.0)
        totals = lax.optimization_barrier(jnp.sum(weights, axis=-1))
        rounded = lax.optimization_barrier((weights * value_factor[:, None, None, :]).astype(jnp.bfloat16))
        scaled = rounded.astype(jnp.float32)
        attended = jnp.einsum('gjrt,tgd->rgjd', scaled, value_rows) / jnp.transpose(totals, (2, 0, 1))[..., None]
        return attended.astype(jnp.bfloat16).reshape(QBLOCK, Q_HEADS * HEAD_DIM)
    attention = lax.map(one_block, (queries, lists, lengths)).reshape(ROWS, Q_HEADS * HEAD_DIM)
    updated = jnp.dot(attention, output_weight, preferred_element_type=jnp.float32) + inputs
    return updated.astype(jnp.bfloat16)

def reference(hidden, norm_gain, w_query, query_gain, w_output, key_cache, value_cache, key_scale, value_scale, page_table, page_tokens, page_list, list_len):
    results = []
    for section_id in range(N_SECTIONS):
        results.append(one_section(hidden[section_id], norm_gain[section_id], w_query[section_id], query_gain[section_id], w_output[section_id], key_cache[section_id], value_cache[section_id], key_scale[section_id], value_scale[section_id], page_table, page_tokens, page_list[section_id], list_len[section_id]))
    stacked = jnp.stack(results, axis=0)
    return jnp.roll(stacked, 1, axis=0)
```

```python
import functools
import math

import jax
import jax.numpy as jnp
from jax import lax
from jax.experimental import pallas as pl
from jax.experimental.pallas import tpu as pltpu
from jax.sharding import PartitionSpec as P

MOST = 8


tiny_eps = 1e-06
masked_score = -1e30
lowest_top = -1e29


def shifted(block, axis, distance):
    devices = range(lax.axis_size(axis))
    route = [((i - distance) % len(devices), i) for i in devices]
    return lax.ppermute(block, axis, route)


def lookup(entries, table):
    places = jnp.arange(table.shape[0], dtype=jnp.int32)
    matches = (entries[..., None] == places).astype(jnp.int32)
    return jnp.sum(matches * table, axis=-1)


def plan_pages(slots, counts, length, target, pages_dev):
    listed = slots.shape[-1]
    order = jnp.arange(listed, dtype=jnp.int32)
    chosen = (slots // pages_dev == target) & (order < length)
    flags = chosen.astype(jnp.int32)
    ranks = jnp.cumsum(flags) - flags
    wanted = jnp.arange(MOST, dtype=jnp.int32)
    picks = ((ranks[None, :] == wanted[:, None]) & chosen[None, :]).astype(jnp.int32)
    local = jnp.sum(picks * (slots % pages_dev)[None, :], axis=1)
    filled = jnp.sum(picks * counts[None, :], axis=1)
    return (local, filled)


def plan_blocks(slots, counts, lengths, target, pages_dev):
    return jax.vmap(
        lambda one_slots, one_counts, one_length: plan_pages(
            one_slots, one_counts, one_length, target, pages_dev
        )
    )(slots, counts, lengths)


def query_kernel(where_ref, mine_ref, other_ref, weight_ref, gain_ref, out_ref, rows_ref):
    half = mine_ref.shape[0]
    head_size = gain_ref.shape[1]

    @pl.when(pl.program_id(0) == 0)
    def _():
        rows_ref[pl.ds(pl.multiple_of(where_ref[0] * half, half), half), :] = mine_ref[...]
        rows_ref[pl.ds(pl.multiple_of((1 - where_ref[0]) * half, half), half), :] = other_ref[...]

    projected = jnp.dot(rows_ref[...], weight_ref[0], preferred_element_type=jnp.float32)
    for head in range(out_ref.shape[0]):
        part = projected[:, head * head_size : (head + 1) * head_size]
        inverse = lax.rsqrt(jnp.mean(part * part, axis=-1, keepdims=True) + tiny_eps)
        scaled = part * inverse * gain_ref[...] / math.sqrt(head_size)
        out_ref[head] = scaled.astype(jnp.bfloat16)


def make_queries(own_half, mine, other, w_query, query_gain):
    half, model_width = mine.shape
    head_size = query_gain.shape[1]
    columns = w_query.shape[2]
    tile = min(512, columns)
    per_tile = tile // head_size
    return pl.pallas_call(
        query_kernel,
        out_shape=jax.ShapeDtypeStruct((columns // head_size, 2 * half, head_size), jnp.bfloat16),
        grid_spec=pltpu.PrefetchScalarGridSpec(
            num_scalar_prefetch=1,
            grid=(columns // tile,),
            in_specs=[
                pl.BlockSpec((half, model_width), lambda i, w: (0, 0)),
                pl.BlockSpec((half, model_width), lambda i, w: (0, 0)),
                pl.BlockSpec((1, model_width, tile), lambda i, w: (0, 0, i)),
                pl.BlockSpec((1, head_size), lambda i, w: (0, 0)),
            ],
            out_specs=pl.BlockSpec((per_tile, 2 * half, head_size), lambda i, w: (i, 0, 0)),
            scratch_shapes=[pltpu.VMEM((2 * half, model_width), jnp.bfloat16)],
        ),
        cost_estimate=pl.CostEstimate(
            flops=4 * half * model_width * columns,
            bytes_accessed=2 * model_width * columns,
            transcendentals=0,
        ),
        name="queries",
    )(own_half, mine, other, w_query, query_gain)


def attend_kernel(kv_local, first_ref, slot_ref, live_ref, q_ref, key_ref, value_ref, factor_ref, acc_ref, lse_ref):
    heads_local, rows, head_size = q_ref.shape
    group_size = heads_local // kv_local
    most = slot_ref.shape[1]
    page_len = key_ref.shape[2]
    block = first_ref[0] + pl.program_id(0)
    live = live_ref[block]
    lanes = lax.broadcasted_iota(jnp.int32, (rows, 128), 1)
    together = 2

    def run(pages):
        span = pages * page_len
        keeper = factor_ref[0, 2 * kv_local : 2 * kv_local + 1, :span] > 0.5
        lse_tile = jnp.full((rows, 128), masked_score, jnp.float32)
        for g in range(kv_local):
            columns = slice(g * head_size, (g + 1) * head_size)
            keys = jnp.concatenate(
                [key_ref[0, slot_ref[block, i], :, columns] for i in range(pages)], axis=0
            )
            values = jnp.concatenate(
                [value_ref[0, slot_ref[block, i], :, columns] for i in range(pages)], axis=0
            )
            key_factor = factor_ref[0, g : g + 1, :span]
            value_factor = factor_ref[0, kv_local + g : kv_local + g + 1, :span]
            for j in range(0, group_size, together):
                head = g * group_size + j
                queries = q_ref[head : head + together].reshape(together * rows, head_size)
                scores = lax.dot_general(
                    queries, keys, (((1,), (1,)), ((), ())), preferred_element_type=jnp.float32
                )
                scores = jnp.where(keeper, scores * key_factor, masked_score)
                top = jnp.maximum(jnp.max(scores, axis=-1, keepdims=True), lowest_top)
                weights = jnp.exp(scores - top)
                total = jnp.sum(weights, axis=-1, keepdims=True)
                scaled = (weights * value_factor).astype(jnp.bfloat16)
                acc = jnp.dot(scaled, values, preferred_element_type=jnp.float32)
                some = total > 0.0
                acc = acc / jnp.where(some, total, 1.0)
                lse = jnp.where(some, top + jnp.log(jnp.where(some, total, 1.0)), masked_score)
                for k in range(together):
                    own = slice(k * rows, (k + 1) * rows)
                    acc_ref[:, (head + k) * head_size : (head + k + 1) * head_size] = acc[own]
                    lse_tile = jnp.where(lanes == head + k, lse[own], lse_tile)
        lse_ref[...] = lse_tile.T[:heads_local, :]

    @pl.when(live <= most // 2)
    def _():
        run(most // 2)

    @pl.when(live > most // 2)
    def _():
        run(most)


def attend(first_block, slots, live_pages, queries, key_cache, value_cache, factors, kv_local, blocks):
    heads_local, rows, head_size = queries.shape
    block_rows = rows // blocks
    cache_spec = pl.BlockSpec(key_cache.shape, lambda b, *_: (0, 0, 0, 0))
    span = factors.shape[2]
    return pl.pallas_call(
        lambda *refs: attend_kernel(kv_local, *refs),
        out_shape=(
            jax.ShapeDtypeStruct((rows, heads_local * head_size), jnp.float32),
            jax.ShapeDtypeStruct((heads_local, rows), jnp.float32),
        ),
        grid_spec=pltpu.PrefetchScalarGridSpec(
            num_scalar_prefetch=3,
            grid=(blocks,),
            in_specs=[
                pl.BlockSpec((heads_local, block_rows, head_size), lambda b, *_: (0, b, 0)),
                cache_spec,
                cache_spec,
                pl.BlockSpec((1,) + factors.shape[1:], lambda b, f, s, l: (f[0] + b, 0, 0)),
            ],
            out_specs=(
                pl.BlockSpec((block_rows, heads_local * head_size), lambda b, *_: (b, 0)),
                pl.BlockSpec((heads_local, block_rows), lambda b, *_: (0, b)),
            ),
        ),
        cost_estimate=pl.CostEstimate(
            flops=4 * rows * heads_local * head_size * span,
            bytes_accessed=2 * key_cache.size * 2,
            transcendentals=rows * heads_local * span,
        ),
        name="attend",
    )(first_block, slots, live_pages, queries, key_cache, value_cache, factors)


def output_kernel(side_ref, acc_ref, share_ref, weight_ref, out_ref, rows_ref):
    heads_local = share_ref.shape[1]
    head_size = acc_ref.shape[1] // heads_local

    @pl.when(pl.program_id(0) == 0)
    def _():
        for head in range(heads_local):
            columns = slice(head * head_size, (head + 1) * head_size)
            rows_ref[:, columns] = (acc_ref[:, columns] * share_ref[:, head : head + 1]).astype(
                jnp.bfloat16
            )

    out_ref[...] = jnp.dot(
        rows_ref[...], weight_ref[0], preferred_element_type=jnp.float32
    ).astype(out_ref.dtype)


def project_out(side, acc, share, w_output, out_type):
    rows, depth = acc.shape
    half_width = w_output.shape[2] // 2
    tile = min(512, half_width)
    steps = half_width // tile
    return pl.pallas_call(
        output_kernel,
        out_shape=jax.ShapeDtypeStruct((rows, half_width), out_type),
        grid_spec=pltpu.PrefetchScalarGridSpec(
            num_scalar_prefetch=1,
            grid=(steps,),
            in_specs=[
                pl.BlockSpec((rows, depth), lambda i, s: (0, 0)),
                pl.BlockSpec(share.shape, lambda i, s: (0, 0)),
                pl.BlockSpec((1, depth, tile), lambda i, s: (0, 0, s[0] * steps + i)),
            ],
            out_specs=pl.BlockSpec((rows, tile), lambda i, s: (0, i)),
            scratch_shapes=[pltpu.VMEM((rows, depth), jnp.bfloat16)],
        ),
        cost_estimate=pl.CostEstimate(
            flops=2 * rows * depth * half_width,
            bytes_accessed=2 * depth * half_width + 4 * rows * depth,
            transcendentals=0,
        ),
        name="project_out",
    )(side, acc, share, w_output)


def body(
    hidden,
    norm_gain,
    w_query,
    query_gain,
    w_output,
    key_cache,
    value_cache,
    key_scale,
    value_scale,
    page_table,
    page_tokens,
    page_list,
    list_len,
):
    row_count = hidden.shape[1]
    head_size = query_gain.shape[1]
    kv_local = key_scale.shape[2]
    pages_dev, page_len = key_cache.shape[1:3]
    count = lax.axis_size("cache")
    own_shard = lax.axis_index("cache")
    own_half = lax.axis_index("heads")
    blocks = page_list.shape[1] // count
    half = row_count // 2
    swap = [(0, 1), (1, 0)]
    ring = [(i, (i + 1) % count) for i in range(count)]
    side = own_half.astype(jnp.int32)[None]
    inputs = hidden[0].astype(jnp.float32)
    inverse = lax.rsqrt(jnp.mean(inputs * inputs, axis=-1, keepdims=True) + tiny_eps)
    normed = (inputs * inverse * norm_gain[0]).astype(jnp.bfloat16)
    mine = lax.dynamic_slice_in_dim(normed, own_half * half, half, 0)
    other = lax.dynamic_slice_in_dim(normed, (1 - own_half) * half, half, 0)

    all_slots = lookup(page_list[0], page_table)
    all_counts = lookup(page_list[0], page_tokens)
    local_all, filled_all = plan_blocks(all_slots, all_counts, list_len[0], own_shard, pages_dev)
    live_pages = jnp.sum((filled_all > 0).astype(jnp.int32), axis=1)
    page_ids = jnp.arange(pages_dev, dtype=jnp.int32)
    picks = local_all[..., None] == page_ids

    def factor(scales):
        picked = jnp.sum(jnp.where(picks[:, None], scales[0].T[None, :, None, :], 0.0), axis=-1)
        return jnp.repeat(picked, page_len, axis=2)

    within = jnp.arange(page_len, dtype=jnp.int32)
    live_mask = (within < filled_all[..., None]).astype(jnp.float32)
    live_mask = live_mask.reshape(live_mask.shape[0], 1, -1)
    factors = jnp.concatenate([factor(key_scale), factor(value_scale), live_mask], axis=1)

    accs, lses = [], []
    for step in range(count):
        if step > 0:
            mine = lax.ppermute(mine, "cache", ring)
            other = lax.ppermute(mine, "heads", swap)
        queries = make_queries(side, mine, other, w_query, query_gain)
        owner = lax.rem(own_shard - step + count, count).astype(jnp.int32)
        acc, lse = attend(
            (owner * blocks)[None], local_all, live_pages, queries, key_cache, value_cache, factors, kv_local, blocks
        )
        accs.append(acc)
        lses.append(lse)

    early = jnp.stack(lses[:-1])
    received = [lses]
    for distance in range(1, count):
        route = [(i, (i + distance) % count) for i in range(count)]
        first = lax.ppermute(early, "cache", route)
        last = lax.ppermute(lses[-1], "cache", route)
        received.append([first[i] for i in range(count - 1)] + [last])
    shares = []
    for step in range(count):
        terms = [received[k][(step - k) % count] for k in range(count)]
        top = functools.reduce(jnp.maximum, terms)
        total = sum(jnp.exp(term - top) for term in terms)
        shares.append((jnp.exp(lses[step] - top) / total).T)

    carry = None
    half_width = w_output.shape[2] // 2
    for step in list(range(1, count)) + [0]:
        away = project_out(1 - side, accs[step], shares[step], w_output, jnp.bfloat16)
        near = project_out(side, accs[step], shares[step], w_output, jnp.float32)
        partial_value = near + lax.ppermute(away, "heads", swap).astype(jnp.float32)
        if carry is not None:
            partial_value = partial_value + carry.astype(jnp.float32)
        if step > 0:
            carry = lax.ppermute(partial_value.astype(jnp.bfloat16), "cache", ring)
    residual = lax.dynamic_slice_in_dim(inputs, own_half * half_width, half_width, 1)
    result = (partial_value + residual).astype(jnp.bfloat16)
    return shifted(result[None], "sections", 1)


def solution(mesh):
    return jax.shard_map(
        body,
        mesh=mesh,
        in_specs=(
            P("sections", "cache", None),
            P("sections", None),
            P("sections", None, "heads"),
            P("sections", None),
            P("sections", "heads", None),
            P("sections", "cache", None, "heads"),
            P("sections", "cache", None, "heads"),
            P("sections", "cache", "heads"),
            P("sections", "cache", "heads"),
            P(),
            P(),
            P("sections", None, None),
            P("sections", None),
        ),
        out_specs=P("sections", "cache", "heads"),
        check_vma=False,
    )
```

```python
import functools
import math

import jax
import jax.numpy as jnp
from jax import lax
from jax.experimental import pallas as pl
from jax.experimental.pallas import tpu as pltpu
from jax.sharding import PartitionSpec as P

MOST = 8


tiny_eps = 1e-06
masked_score = -1e30
lowest_top = -1e29


def shifted(block, axis, distance):
    devices = range(lax.axis_size(axis))
    route = [((i - distance) % len(devices), i) for i in devices]
    return lax.ppermute(block, axis, route)


def lookup(entries, table):
    places = jnp.arange(table.shape[0], dtype=jnp.int32)
    matches = (entries[..., None] == places).astype(jnp.int32)
    return jnp.sum(matches * table, axis=-1)


def plan_pages(slots, counts, length, target, pages_dev):
    listed = slots.shape[-1]
    order = jnp.arange(listed, dtype=jnp.int32)
    chosen = (slots // pages_dev == target) & (order < length)
    flags = chosen.astype(jnp.int32)
    ranks = jnp.cumsum(flags) - flags
    wanted = jnp.arange(MOST, dtype=jnp.int32)
    picks = ((ranks[None, :] == wanted[:, None]) & chosen[None, :]).astype(jnp.int32)
    local = jnp.sum(picks * (slots % pages_dev)[None, :], axis=1)
    filled = jnp.sum(picks * counts[None, :], axis=1)
    return (local, filled)


def plan_blocks(slots, counts, lengths, target, pages_dev):
    return jax.vmap(
        lambda one_slots, one_counts, one_length: plan_pages(
            one_slots, one_counts, one_length, target, pages_dev
        )
    )(slots, counts, lengths)


def query_kernel(where_ref, mine_ref, other_ref, weight_ref, gain_ref, out_ref, rows_ref):
    half = mine_ref.shape[0]
    head_size = gain_ref.shape[1]

    @pl.when(pl.program_id(0) == 0)
    def _():
        rows_ref[pl.ds(pl.multiple_of(where_ref[0] * half, half), half), :] = mine_ref[...]
        rows_ref[pl.ds(pl.multiple_of((1 - where_ref[0]) * half, half), half), :] = other_ref[...]

    projected = jnp.dot(rows_ref[...], weight_ref[0], preferred_element_type=jnp.float32)
    for head in range(out_ref.shape[0]):
        part = projected[:, head * head_size : (head + 1) * head_size]
        inverse = lax.rsqrt(jnp.mean(part * part, axis=-1, keepdims=True) + tiny_eps)
        scaled = part * inverse * gain_ref[...] / math.sqrt(head_size)
        out_ref[head] = scaled.astype(jnp.bfloat16)


def make_queries(own_half, mine, other, w_query, query_gain):
    half, model_width = mine.shape
    head_size = query_gain.shape[1]
    columns = w_query.shape[2]
    tile = min(512, columns)
    per_tile = tile // head_size
    return pl.pallas_call(
        query_kernel,
        out_shape=jax.ShapeDtypeStruct((columns // head_size, 2 * half, head_size), jnp.bfloat16),
        grid_spec=pltpu.PrefetchScalarGridSpec(
            num_scalar_prefetch=1,
            grid=(columns // tile,),
            in_specs=[
                pl.BlockSpec((half, model_width), lambda i, w: (0, 0)),
                pl.BlockSpec((half, model_width), lambda i, w: (0, 0)),
                pl.BlockSpec((1, model_width, tile), lambda i, w: (0, 0, i)),
                pl.BlockSpec((1, head_size), lambda i, w: (0, 0)),
            ],
            out_specs=pl.BlockSpec((per_tile, 2 * half, head_size), lambda i, w: (i, 0, 0)),
            scratch_shapes=[pltpu.VMEM((2 * half, model_width), jnp.bfloat16)],
        ),
        cost_estimate=pl.CostEstimate(
            flops=4 * half * model_width * columns,
            bytes_accessed=2 * model_width * columns,
            transcendentals=0,
        ),
        name="queries",
    )(own_half, mine, other, w_query, query_gain)


def attend_kernel(kv_local, first_ref, slot_ref, live_ref, q_ref, key_ref, value_ref, factor_ref, acc_ref, lse_ref):
    heads_local, rows, head_size = q_ref.shape
    group_size = heads_local // kv_local
    most = slot_ref.shape[1]
    page_len = key_ref.shape[2]
    block = first_ref[0] + pl.program_id(0)
    live = live_ref[block]
    lanes = lax.broadcasted_iota(jnp.int32, (rows, 128), 1)
    together = 2

    def run(pages):
        span = pages * page_len
        keeper = factor_ref[0, 2 * kv_local : 2 * kv_local + 1, :span] > 0.5
        lse_tile = jnp.full((rows, 128), masked_score, jnp.float32)
        for g in range(kv_local):
            columns = slice(g * head_size, (g + 1) * head_size)
            keys = jnp.concatenate(
                [key_ref[0, slot_ref[block, i], :, columns] for i in range(pages)], axis=0
            )
            values = jnp.concatenate(
                [value_ref[0, slot_ref[block, i], :, columns] for i in range(pages)], axis=0
            )
            key_factor = factor_ref[0, g : g + 1, :span]
            value_factor = factor_ref[0, kv_local + g : kv_local + g + 1, :span]
            for j in range(0, group_size, together):
                head = g * group_size + j
                queries = q_ref[head : head + together].reshape(together * rows, head_size)
                scores = lax.dot_general(
                    queries, keys, (((1,), (1,)), ((), ())), preferred_element_type=jnp.float32
                )
                scores = jnp.where(keeper, scores * key_factor, masked_score)
                top = jnp.maximum(jnp.max(scores, axis=-1, keepdims=True), lowest_top)
                weights = jnp.exp(scores - top)
                total = jnp.sum(weights, axis=-1, keepdims=True)
                scaled = (weights * value_factor).astype(jnp.bfloat16)
                acc = jnp.dot(scaled, values, preferred_element_type=jnp.float32)
                some = total > 0.0
                acc = acc / jnp.where(some, total, 1.0)
                lse = jnp.where(some, top + jnp.log(jnp.where(some, total, 1.0)), masked_score)
                for k in range(together):
                    own = slice(k * rows, (k + 1) * rows)
                    acc_ref[:, (head + k) * head_size : (head + k + 1) * head_size] = acc[own]
                    lse_tile = jnp.where(lanes == head + k, lse[own], lse_tile)
        lse_ref[...] = lse_tile.T[:heads_local, :]

    @pl.when(live <= most // 2)
    def _():
        run(most // 2)

    @pl.when(live > most // 2)
    def _():
        run(most)


def attend(first_block, slots, live_pages, queries, key_cache, value_cache, factors, kv_local, blocks):
    heads_local, rows, head_size = queries.shape
    block_rows = rows // blocks
    cache_spec = pl.BlockSpec(key_cache.shape, lambda b, *_: (0, 0, 0, 0))
    span = factors.shape[2]
    return pl.pallas_call(
        lambda *refs: attend_kernel(kv_local, *refs),
        out_shape=(
            jax.ShapeDtypeStruct((rows, heads_local * head_size), jnp.float32),
            jax.ShapeDtypeStruct((heads_local, rows), jnp.float32),
        ),
        grid_spec=pltpu.PrefetchScalarGridSpec(
            num_scalar_prefetch=3,
            grid=(blocks,),
            in_specs=[
                pl.BlockSpec((heads_local, block_rows, head_size), lambda b, *_: (0, b, 0)),
                cache_spec,
                cache_spec,
                pl.BlockSpec((1,) + factors.shape[1:], lambda b, f, s, l: (f[0] + b, 0, 0)),
            ],
            out_specs=(
                pl.BlockSpec((block_rows, heads_local * head_size), lambda b, *_: (b, 0)),
                pl.BlockSpec((heads_local, block_rows), lambda b, *_: (0, b)),
            ),
        ),
        cost_estimate=pl.CostEstimate(
            flops=4 * rows * heads_local * head_size * span,
            bytes_accessed=2 * key_cache.size * 2,
            transcendentals=rows * heads_local * span,
        ),
        name="attend",
    )(first_block, slots, live_pages, queries, key_cache, value_cache, factors)


def output_kernel(side_ref, acc_ref, share_ref, weight_ref, out_ref, rows_ref):
    heads_local = share_ref.shape[1]
    head_size = acc_ref.shape[1] // heads_local

    @pl.when(pl.program_id(0) == 0)
    def _():
        for head in range(heads_local):
            columns = slice(head * head_size, (head + 1) * head_size)
            rows_ref[:, columns] = (acc_ref[:, columns] * share_ref[:, head : head + 1]).astype(
                jnp.bfloat16
            )

    out_ref[...] = jnp.dot(
        rows_ref[...], weight_ref[0], preferred_element_type=jnp.float32
    ).astype(out_ref.dtype)


def project_out(side, acc, share, w_output, out_type):
    rows, depth = acc.shape
    half_width = w_output.shape[2] // 2
    tile = min(512, half_width)
    steps = half_width // tile
    return pl.pallas_call(
        output_kernel,
        out_shape=jax.ShapeDtypeStruct((rows, half_width), out_type),
        grid_spec=pltpu.PrefetchScalarGridSpec(
            num_scalar_prefetch=1,
            grid=(steps,),
            in_specs=[
                pl.BlockSpec((rows, depth), lambda i, s: (0, 0)),
                pl.BlockSpec(share.shape, lambda i, s: (0, 0)),
                pl.BlockSpec((1, depth, tile), lambda i, s: (0, 0, s[0] * steps + i)),
            ],
            out_specs=pl.BlockSpec((rows, tile), lambda i, s: (0, i)),
            scratch_shapes=[pltpu.VMEM((rows, depth), jnp.bfloat16)],
        ),
        cost_estimate=pl.CostEstimate(
            flops=2 * rows * depth * half_width,
            bytes_accessed=2 * depth * half_width + 4 * rows * depth,
            transcendentals=0,
        ),
        name="project_out",
    )(side, acc, share, w_output)


def exchange_kernel(count, own_ref, out_ref, send_sems, receive_sems):
    own = lax.axis_index("cache")
    barrier = pltpu.get_barrier_semaphore()
    for distance in range(1, count):
        pl.semaphore_signal(
            barrier,
            inc=1,
            device_id={"cache": lax.rem(own + distance, count)},
            device_id_type=pl.DeviceIdType.MESH,
        )
    pl.semaphore_wait(barrier, count - 1)
    copies = []
    for distance in range(1, count):
        copy = pltpu.make_async_remote_copy(
            src_ref=own_ref,
            dst_ref=out_ref.at[distance - 1],
            send_sem=send_sems.at[distance - 1],
            recv_sem=receive_sems.at[distance - 1],
            device_id={"cache": lax.rem(own + distance, count)},
            device_id_type=pl.DeviceIdType.MESH,
        )
        copy.start()
        copies.append(copy)
    for copy in copies:
        copy.wait()


def exchange(own, count):
    held = pl.BlockSpec(memory_space=pltpu.VMEM)
    return pl.pallas_call(
        functools.partial(exchange_kernel, count),
        out_shape=jax.ShapeDtypeStruct((count - 1,) + own.shape, own.dtype),
        in_specs=[held],
        out_specs=held,
        scratch_shapes=[
            pltpu.SemaphoreType.DMA((count - 1,)),
            pltpu.SemaphoreType.DMA((count - 1,)),
        ],
        compiler_params=pltpu.CompilerParams(collective_id=0, has_side_effects=True),
        name="exchange",
    )(own)


def body(
    hidden,
    norm_gain,
    w_query,
    query_gain,
    w_output,
    key_cache,
    value_cache,
    key_scale,
    value_scale,
    page_table,
    page_tokens,
    page_list,
    list_len,
):
    row_count = hidden.shape[1]
    head_size = query_gain.shape[1]
    kv_local = key_scale.shape[2]
    pages_dev, page_len = key_cache.shape[1:3]
    count = lax.axis_size("cache")
    own_shard = lax.axis_index("cache")
    own_half = lax.axis_index("heads")
    blocks = page_list.shape[1] // count
    half = row_count // 2
    swap = [(0, 1), (1, 0)]
    ring = [(i, (i + 1) % count) for i in range(count)]
    side = own_half.astype(jnp.int32)[None]
    inputs = hidden[0].astype(jnp.float32)
    inverse = lax.rsqrt(jnp.mean(inputs * inputs, axis=-1, keepdims=True) + tiny_eps)
    normed = (inputs * inverse * norm_gain[0]).astype(jnp.bfloat16)
    mine = lax.dynamic_slice_in_dim(normed, own_half * half, half, 0)
    other = lax.dynamic_slice_in_dim(normed, (1 - own_half) * half, half, 0)

    all_slots = lookup(page_list[0], page_table)
    all_counts = lookup(page_list[0], page_tokens)
    local_all, filled_all = plan_blocks(all_slots, all_counts, list_len[0], own_shard, pages_dev)
    live_pages = jnp.sum((filled_all > 0).astype(jnp.int32), axis=1)
    page_ids = jnp.arange(pages_dev, dtype=jnp.int32)
    picks = local_all[..., None] == page_ids

    def factor(scales):
        picked = jnp.sum(jnp.where(picks[:, None], scales[0].T[None, :, None, :], 0.0), axis=-1)
        return jnp.repeat(picked, page_len, axis=2)

    within = jnp.arange(page_len, dtype=jnp.int32)
    live_mask = (within < filled_all[..., None]).astype(jnp.float32)
    live_mask = live_mask.reshape(live_mask.shape[0], 1, -1)
    factors = jnp.concatenate([factor(key_scale), factor(value_scale), live_mask], axis=1)

    accs, lses = [], []
    for step in range(count):
        if step > 0:
            mine = lax.ppermute(mine, "cache", ring)
            mine, lses[-1] = lax.optimization_barrier((mine, lses[-1]))
            other = lax.ppermute(mine, "heads", swap)
        queries = make_queries(side, mine, other, w_query, query_gain)
        owner = lax.rem(own_shard - step + count, count).astype(jnp.int32)
        acc, lse = attend(
            (owner * blocks)[None], local_all, live_pages, queries, key_cache, value_cache, factors, kv_local, blocks
        )
        accs.append(acc)
        lses.append(lse)

    gathered = exchange(jnp.stack(lses), count)
    received = [lses] + [[gathered[k, i] for i in range(count)] for k in range(count - 1)]
    shares = []
    for step in range(count):
        terms = [received[k][(step - k) % count] for k in range(count)]
        top = functools.reduce(jnp.maximum, terms)
        total = sum(jnp.exp(term - top) for term in terms)
        shares.append((jnp.exp(lses[step] - top) / total).T)

    carry = None
    half_width = w_output.shape[2] // 2
    for step in list(range(1, count)) + [0]:
        away = project_out(1 - side, accs[step], shares[step], w_output, jnp.bfloat16)
        near = project_out(side, accs[step], shares[step], w_output, jnp.float32)
        partial_value = near + lax.ppermute(away, "heads", swap).astype(jnp.float32)
        if carry is not None:
            partial_value = partial_value + carry.astype(jnp.float32)
        if step > 0:
            carry = lax.ppermute(partial_value.astype(jnp.bfloat16), "cache", ring)
    residual = lax.dynamic_slice_in_dim(inputs, own_half * half_width, half_width, 1)
    result = (partial_value + residual).astype(jnp.bfloat16)
    return shifted(result[None], "sections", 1)


def solution(mesh):
    return jax.shard_map(
        body,
        mesh=mesh,
        in_specs=(
            P("sections", "cache", None),
            P("sections", None),
            P("sections", None, "heads"),
            P("sections", None),
            P("sections", "heads", None),
            P("sections", "cache", None, "heads"),
            P("sections", "cache", None, "heads"),
            P("sections", "cache", "heads"),
            P("sections", "cache", "heads"),
            P(),
            P(),
            P("sections", None, None),
            P("sections", None),
        ),
        out_specs=P("sections", "cache", "heads"),
        check_vma=False,
    )
```

```python
import functools
import math

import jax
import jax.numpy as jnp
from jax import lax
from jax.experimental import pallas as pl
from jax.experimental.pallas import tpu as pltpu
from jax.sharding import PartitionSpec as P

MOST = 8


tiny_eps = 1e-06
masked_score = -1e30
lowest_top = -1e29


def shifted(block, axis, distance):
    devices = range(lax.axis_size(axis))
    route = [((i - distance) % len(devices), i) for i in devices]
    return lax.ppermute(block, axis, route)


def lookup(entries, table):
    places = jnp.arange(table.shape[0], dtype=jnp.int32)
    matches = (entries[..., None] == places).astype(jnp.int32)
    return jnp.sum(matches * table, axis=-1)


def plan_pages(slots, counts, length, target, pages_dev):
    listed = slots.shape[-1]
    order = jnp.arange(listed, dtype=jnp.int32)
    chosen = (slots // pages_dev == target) & (order < length)
    flags = chosen.astype(jnp.int32)
    ranks = jnp.cumsum(flags) - flags
    wanted = jnp.arange(MOST, dtype=jnp.int32)
    picks = ((ranks[None, :] == wanted[:, None]) & chosen[None, :]).astype(jnp.int32)
    local = jnp.sum(picks * (slots % pages_dev)[None, :], axis=1)
    filled = jnp.sum(picks * counts[None, :], axis=1)
    return (local, filled)


def plan_blocks(slots, counts, lengths, target, pages_dev):
    return jax.vmap(
        lambda one_slots, one_counts, one_length: plan_pages(
            one_slots, one_counts, one_length, target, pages_dev
        )
    )(slots, counts, lengths)


def query_kernel(where_ref, mine_ref, other_ref, weight_ref, gain_ref, out_ref, rows_ref):
    half = mine_ref.shape[0]
    head_size = gain_ref.shape[1]

    @pl.when(pl.program_id(0) == 0)
    def _():
        rows_ref[pl.ds(pl.multiple_of(where_ref[0] * half, half), half), :] = mine_ref[...]
        rows_ref[pl.ds(pl.multiple_of((1 - where_ref[0]) * half, half), half), :] = other_ref[...]

    projected = jnp.dot(rows_ref[...], weight_ref[0], preferred_element_type=jnp.float32)
    for head in range(out_ref.shape[0]):
        part = projected[:, head * head_size : (head + 1) * head_size]
        inverse = lax.rsqrt(jnp.mean(part * part, axis=-1, keepdims=True) + tiny_eps)
        scaled = part * inverse * gain_ref[...] / math.sqrt(head_size)
        out_ref[head] = scaled.astype(jnp.bfloat16)


def make_queries(own_half, mine, other, w_query, query_gain):
    half, model_width = mine.shape
    head_size = query_gain.shape[1]
    columns = w_query.shape[2]
    tile = min(512, columns)
    per_tile = tile // head_size
    return pl.pallas_call(
        query_kernel,
        out_shape=jax.ShapeDtypeStruct((columns // head_size, 2 * half, head_size), jnp.bfloat16),
        grid_spec=pltpu.PrefetchScalarGridSpec(
            num_scalar_prefetch=1,
            grid=(columns // tile,),
            in_specs=[
                pl.BlockSpec((half, model_width), lambda i, w: (0, 0)),
                pl.BlockSpec((half, model_width), lambda i, w: (0, 0)),
                pl.BlockSpec((1, model_width, tile), lambda i, w: (0, 0, i)),
                pl.BlockSpec((1, head_size), lambda i, w: (0, 0)),
            ],
            out_specs=pl.BlockSpec((per_tile, 2 * half, head_size), lambda i, w: (i, 0, 0)),
            scratch_shapes=[pltpu.VMEM((2 * half, model_width), jnp.bfloat16)],
        ),
        cost_estimate=pl.CostEstimate(
            flops=4 * half * model_width * columns,
            bytes_accessed=2 * model_width * columns,
            transcendentals=0,
        ),
        name="queries",
    )(own_half, mine, other, w_query, query_gain)


def attend_kernel(kv_local, first_ref, slot_ref, live_ref, q_ref, key_ref, value_ref, factor_ref, acc_ref, lse_ref):
    heads_local, rows, head_size = q_ref.shape
    group_size = heads_local // kv_local
    most = slot_ref.shape[1]
    page_len = key_ref.shape[2]
    block = first_ref[0] + pl.program_id(0)
    live = live_ref[block]
    lanes = lax.broadcasted_iota(jnp.int32, (rows, 128), 1)
    together = 2

    def run(pages):
        span = pages * page_len
        keeper = factor_ref[0, 2 * kv_local : 2 * kv_local + 1, :span] > 0.5
        lse_tile = jnp.full((rows, 128), masked_score, jnp.float32)
        for g in range(kv_local):
            columns = slice(g * head_size, (g + 1) * head_size)
            keys = jnp.concatenate(
                [key_ref[0, slot_ref[block, i], :, columns] for i in range(pages)], axis=0
            )
            values = jnp.concatenate(
                [value_ref[0, slot_ref[block, i], :, columns] for i in range(pages)], axis=0
            )
            key_factor = factor_ref[0, g : g + 1, :span]
            value_factor = factor_ref[0, kv_local + g : kv_local + g + 1, :span]
            for j in range(0, group_size, together):
                head = g * group_size + j
                queries = q_ref[head : head + together].reshape(together * rows, head_size)
                scores = lax.dot_general(
                    queries, keys, (((1,), (1,)), ((), ())), preferred_element_type=jnp.float32
                )
                scores = jnp.where(keeper, scores * key_factor, masked_score)
                top = jnp.maximum(jnp.max(scores, axis=-1, keepdims=True), lowest_top)
                weights = jnp.exp(scores - top)
                total = jnp.sum(weights, axis=-1, keepdims=True)
                scaled = (weights * value_factor).astype(jnp.bfloat16)
                acc = jnp.dot(scaled, values, preferred_element_type=jnp.float32)
                some = total > 0.0
                acc = acc / jnp.where(some, total, 1.0)
                lse = jnp.where(some, top + jnp.log(jnp.where(some, total, 1.0)), masked_score)
                for k in range(together):
                    own = slice(k * rows, (k + 1) * rows)
                    acc_ref[:, (head + k) * head_size : (head + k + 1) * head_size] = acc[own].astype(jnp.bfloat16)
                    lse_tile = jnp.where(lanes == head + k, lse[own], lse_tile)
        lse_ref[...] = lse_tile.T[:heads_local, :]

    @pl.when(live <= most // 2)
    def _():
        run(most // 2)

    @pl.when(live > most // 2)
    def _():
        run(most)


def attend(first_block, slots, live_pages, queries, key_cache, value_cache, factors, kv_local, blocks):
    heads_local, rows, head_size = queries.shape
    block_rows = rows // blocks
    cache_spec = pl.BlockSpec(key_cache.shape, lambda b, *_: (0, 0, 0, 0))
    span = factors.shape[2]
    return pl.pallas_call(
        lambda *refs: attend_kernel(kv_local, *refs),
        out_shape=(
            jax.ShapeDtypeStruct((rows, heads_local * head_size), jnp.bfloat16),
            jax.ShapeDtypeStruct((heads_local, rows), jnp.float32),
        ),
        grid_spec=pltpu.PrefetchScalarGridSpec(
            num_scalar_prefetch=3,
            grid=(blocks,),
            in_specs=[
                pl.BlockSpec((heads_local, block_rows, head_size), lambda b, *_: (0, b, 0)),
                cache_spec,
                cache_spec,
                pl.BlockSpec((1,) + factors.shape[1:], lambda b, f, s, l: (f[0] + b, 0, 0)),
            ],
            out_specs=(
                pl.BlockSpec((block_rows, heads_local * head_size), lambda b, *_: (b, 0)),
                pl.BlockSpec((heads_local, block_rows), lambda b, *_: (0, b)),
            ),
        ),
        cost_estimate=pl.CostEstimate(
            flops=4 * rows * heads_local * head_size * span,
            bytes_accessed=2 * key_cache.size * 2,
            transcendentals=rows * heads_local * span,
        ),
        name="attend",
    )(first_block, slots, live_pages, queries, key_cache, value_cache, factors)


def output_kernel(side_ref, acc_ref, share_ref, weight_ref, away_ref, near_ref, rows_ref):
    heads_local = share_ref.shape[1]
    head_size = acc_ref.shape[1] // heads_local
    steps = pl.num_programs(0) // 2

    @pl.when(pl.program_id(0) == 0)
    def _():
        for head in range(heads_local):
            columns = slice(head * head_size, (head + 1) * head_size)
            rows_ref[:, columns] = (
                acc_ref[:, columns].astype(jnp.float32) * share_ref[:, head : head + 1]
            ).astype(jnp.bfloat16)

    product = jnp.dot(rows_ref[...], weight_ref[0], preferred_element_type=jnp.float32)

    @pl.when(pl.program_id(0) < steps)
    def _():
        away_ref[...] = product.astype(jnp.bfloat16)

    @pl.when(pl.program_id(0) >= steps)
    def _():
        near_ref[...] = product


def project_out(side, acc, share, w_output):
    rows, depth = acc.shape
    half_width = w_output.shape[2] // 2
    tile = min(512, half_width)
    steps = half_width // tile

    def weight_tile(i, s):
        own = jnp.where(i < steps, 1 - s[0], s[0])
        return (0, 0, own * steps + lax.rem(i, steps))

    return pl.pallas_call(
        output_kernel,
        out_shape=(
            jax.ShapeDtypeStruct((rows, half_width), jnp.bfloat16),
            jax.ShapeDtypeStruct((rows, half_width), jnp.float32),
        ),
        grid_spec=pltpu.PrefetchScalarGridSpec(
            num_scalar_prefetch=1,
            grid=(2 * steps,),
            in_specs=[
                pl.BlockSpec((rows, depth), lambda i, s: (0, 0)),
                pl.BlockSpec(share.shape, lambda i, s: (0, 0)),
                pl.BlockSpec((1, depth, tile), weight_tile),
            ],
            out_specs=(
                pl.BlockSpec((rows, tile), lambda i, s: (0, jnp.minimum(i, steps - 1))),
                pl.BlockSpec((rows, tile), lambda i, s: (0, jnp.maximum(i - steps, 0))),
            ),
            scratch_shapes=[pltpu.VMEM((rows, depth), jnp.bfloat16)],
        ),
        cost_estimate=pl.CostEstimate(
            flops=4 * rows * depth * half_width,
            bytes_accessed=4 * depth * half_width + 2 * rows * depth,
            transcendentals=0,
        ),
        name="project_out",
    )(side, acc, share, w_output)


def exchange_kernel(count, own_ref, out_ref, send_sems, receive_sems):
    own = lax.axis_index("cache")
    barrier = pltpu.get_barrier_semaphore()
    for distance in range(1, count):
        pl.semaphore_signal(
            barrier,
            inc=1,
            device_id={"cache": lax.rem(own + distance, count)},
            device_id_type=pl.DeviceIdType.MESH,
        )
    pl.semaphore_wait(barrier, count - 1)
    copies = []
    for distance in range(1, count):
        copy = pltpu.make_async_remote_copy(
            src_ref=own_ref,
            dst_ref=out_ref.at[distance - 1],
            send_sem=send_sems.at[distance - 1],
            recv_sem=receive_sems.at[distance - 1],
            device_id={"cache": lax.rem(own + distance, count)},
            device_id_type=pl.DeviceIdType.MESH,
        )
        copy.start()
        copies.append(copy)
    for copy in copies:
        copy.wait()


def exchange(own, count):
    held = pl.BlockSpec(memory_space=pltpu.VMEM)
    return pl.pallas_call(
        functools.partial(exchange_kernel, count),
        out_shape=jax.ShapeDtypeStruct((count - 1,) + own.shape, own.dtype),
        in_specs=[held],
        out_specs=held,
        scratch_shapes=[
            pltpu.SemaphoreType.DMA((count - 1,)),
            pltpu.SemaphoreType.DMA((count - 1,)),
        ],
        compiler_params=pltpu.CompilerParams(collective_id=0, has_side_effects=True),
        name="exchange",
    )(own)


def body(
    hidden,
    norm_gain,
    w_query,
    query_gain,
    w_output,
    key_cache,
    value_cache,
    key_scale,
    value_scale,
    page_table,
    page_tokens,
    page_list,
    list_len,
):
    row_count = hidden.shape[1]
    head_size = query_gain.shape[1]
    kv_local = key_scale.shape[2]
    pages_dev, page_len = key_cache.shape[1:3]
    count = lax.axis_size("cache")
    own_shard = lax.axis_index("cache")
    own_half = lax.axis_index("heads")
    blocks = page_list.shape[1] // count
    half = row_count // 2
    swap = [(0, 1), (1, 0)]
    ring = [(i, (i + 1) % count) for i in range(count)]
    side = own_half.astype(jnp.int32)[None]
    inputs = hidden[0].astype(jnp.float32)
    inverse = lax.rsqrt(jnp.mean(inputs * inputs, axis=-1, keepdims=True) + tiny_eps)
    normed = (inputs * inverse * norm_gain[0]).astype(jnp.bfloat16)
    mine = lax.dynamic_slice_in_dim(normed, own_half * half, half, 0)
    other = lax.dynamic_slice_in_dim(normed, (1 - own_half) * half, half, 0)

    all_slots = lookup(page_list[0], page_table)
    all_counts = lookup(page_list[0], page_tokens)
    local_all, filled_all = plan_blocks(all_slots, all_counts, list_len[0], own_shard, pages_dev)
    live_pages = jnp.sum((filled_all > 0).astype(jnp.int32), axis=1)
    page_ids = jnp.arange(pages_dev, dtype=jnp.int32)
    picks = local_all[..., None] == page_ids

    def factor(scales):
        picked = jnp.sum(jnp.where(picks[:, None], scales[0].T[None, :, None, :], 0.0), axis=-1)
        return jnp.repeat(picked, page_len, axis=2)

    within = jnp.arange(page_len, dtype=jnp.int32)
    live_mask = (within < filled_all[..., None]).astype(jnp.float32)
    live_mask = live_mask.reshape(live_mask.shape[0], 1, -1)
    factors = jnp.concatenate([factor(key_scale), factor(value_scale), live_mask], axis=1)

    accs, lses = [], []
    for step in range(count):
        if step > 0:
            mine = lax.ppermute(mine, "cache", ring)
            mine, lses[-1] = lax.optimization_barrier((mine, lses[-1]))
            other = lax.ppermute(mine, "heads", swap)
        queries = make_queries(side, mine, other, w_query, query_gain)
        owner = lax.rem(own_shard - step + count, count).astype(jnp.int32)
        acc, lse = attend(
            (owner * blocks)[None], local_all, live_pages, queries, key_cache, value_cache, factors, kv_local, blocks
        )
        accs.append(acc)
        lses.append(lse)

    gathered = exchange(jnp.stack(lses), count)
    received = [lses] + [[gathered[k, i] for i in range(count)] for k in range(count - 1)]
    shares = []
    for step in range(count):
        terms = [received[k][(step - k) % count] for k in range(count)]
        top = functools.reduce(jnp.maximum, terms)
        total = sum(jnp.exp(term - top) for term in terms)
        shares.append((jnp.exp(lses[step] - top) / total).T)

    carry = None
    half_width = w_output.shape[2] // 2
    residual = lax.dynamic_slice_in_dim(inputs, own_half * half_width, half_width, 1)
    for step in list(range(1, count)) + [0]:
        away, near = project_out(side, accs[step], shares[step], w_output)
        partial_value = near + lax.ppermute(away, "heads", swap).astype(jnp.float32)
        if step == 0:
            partial_value = partial_value + residual
            results = []
            for part, rows in zip(carry, (slice(0, half), slice(half, row_count))):
                result = (partial_value[rows] + part.astype(jnp.float32)).astype(jnp.bfloat16)
                partial_value, result = lax.optimization_barrier((partial_value, result))
                results.append(shifted(result, "sections", 1))
            return jnp.concatenate(results, axis=0)[None]
        if carry is not None:
            partial_value = partial_value + carry.astype(jnp.float32)
        carry = partial_value.astype(jnp.bfloat16)
        if step < count - 1:
            carry = lax.ppermute(carry, "cache", ring)
        else:
            upper = lax.ppermute(carry[:half], "cache", ring)
            upper, lower = lax.optimization_barrier((upper, carry[half:]))
            carry = [upper, lax.ppermute(lower, "cache", ring)]


def solution(mesh):
    return jax.shard_map(
        body,
        mesh=mesh,
        in_specs=(
            P("sections", "cache", None),
            P("sections", None),
            P("sections", None, "heads"),
            P("sections", None),
            P("sections", "heads", None),
            P("sections", "cache", None, "heads"),
            P("sections", "cache", None, "heads"),
            P("sections", "cache", "heads"),
            P("sections", "cache", "heads"),
            P(),
            P(),
            P("sections", None, None),
            P("sections", None),
        ),
        out_specs=P("sections", "cache", "heads"),
        check_vma=False,
    )
```
